256 devices in a mesh: tm: 16 (over z, core), panel: 16 (over y, x).
Axes of the slice: x: 4, y: 4, z: 8, core: 2. Of those that a mesh axis runs over, the one named last changes fastest.
Arguments:
- dynamics: bfloat16 [16, 1536, 1536], P('tm', 'panel'), may hold values from -1 to 1
- coupling: bfloat16 [16, 1536, 1536], P('tm', 'panel'), may hold values from -1 to 1
- cost_matrix: bfloat16 [16, 1536, 1536], P('tm', 'panel'), may hold values from -1 to 1
- band_offset: int32 [16, 12], P('tm'), may hold values from -1 to 0
- band_width: int32 [16, 12], P('tm'), may hold values from 2 to 3
Outputs:
- level_one: bfloat16 [16, 3, 1536, 1536], P('tm', None, 'panel')
- level_two: bfloat16 [16, 3, 1536, 1536], P('tm', None, 'panel')
The draws below stay inside these ranges and needn't reach their ends.
All inputs are finite; a program needn't handle non-finite values.
Results may differ from the reference program's by a relative error of at most 0.012.
The reference program's roundings to bfloat16 on the way count: a program that leaves them out, or rounds other values in their place, can miss the bound.
Values may be sent and summed in bfloat16 or wider, within the bound.
A program may use at most 128 MiB of HBM per device.

```python
import jax
import jax.numpy as jnp

NS = 1536
BLOCK = 128
LEVELS = 2
HORIZON = 16
BLOCKS = 12


def rough_matrix(key, diag_lo, diag_hi, off_scale):
    key_diag, key_off = jax.random.split(key)
    shape = (HORIZON, NS, NS)
    off = jnp.clip(jax.random.normal(key_off, shape, jnp.float32), -6.0, 6.0) * off_scale
    diag = jnp.exp(jax.random.uniform(key_diag, shape, jnp.float32, jnp.log(diag_lo), jnp.log(diag_hi)))
    rows = diagonal_mask()
    return jnp.where(rows, diag, off)


def diagonal_mask():
    first = jnp.arange(NS)[:, None]
    second = jnp.arange(NS)[None, :]
    return (first == second)[None]


def draw_dynamics(key, part):
    return rough_matrix(jax.random.fold_in(key, 11), 0.45, 0.95, 0.35 / NS ** 0.5).astype(jnp.bfloat16)


def draw_coupling(key, part):
    return rough_matrix(jax.random.fold_in(key, 23), 0.45, 0.75, 0.15 / BLOCK ** 0.5).astype(jnp.bfloat16)


def draw_cost_matrix(key, part):
    return rough_matrix(jax.random.fold_in(key, 37), 0.45, 0.85, 0.4 / NS ** 0.5).astype(jnp.bfloat16)


def plant(result, stream_key, smallest, top_value):
    shape = result.shape
    index_at = [jax.random.randint(jax.random.fold_in(stream_key, axis), (), 0, shape[axis]) for axis in range(len(shape))]
    result = result.at[tuple(index_at)].set(smallest)
    longest = shape.index(max(shape))
    index_at[longest] = (index_at[longest] + 1) % shape[longest]
    return result.at[tuple(index_at)].set(top_value)


def setup_inputs(seed: int = 0) -> dict:
    key_of = jax.random.split(jax.random.key(seed), 6)
    return {
        "dynamics": draw_dynamics(jax.random.fold_in(key_of[5], 71), 0),
        "coupling": draw_coupling(jax.random.fold_in(key_of[5], 71), 0),
        "cost_matrix": draw_cost_matrix(jax.random.fold_in(key_of[5], 71), 0),
        "band_offset": plant(jax.random.randint(key_of[3], (HORIZON, BLOCKS), -1, 1), jax.random.fold_in(key_of[3], 1), -1, 0).astype(jnp.int32),
        "band_width": plant(jax.random.randint(key_of[4], (HORIZON, BLOCKS), 2, 4), jax.random.fold_in(key_of[4], 1), 2, 3).astype(jnp.int32),
    }


def product(left, right):
    return jnp.einsum("kij,kjl->kil", left.astype(jnp.float32), right.astype(jnp.float32))


def combine(earlier, later):
    a_one, c_one, j_one = earlier
    a_two, c_two, j_two = later
    eye = jnp.eye(NS, dtype=jnp.float32)[None]
    k_mat = product(c_one, j_two).astype(jnp.bfloat16)
    q_mat = product(k_mat, k_mat).astype(jnp.bfloat16)
    k_q = product(k_mat, q_mat)
    x_mat = (eye - k_mat.astype(jnp.float32) + q_mat.astype(jnp.float32) - k_q).astype(jnp.bfloat16)
    u_mat = product(x_mat, a_one).astype(jnp.bfloat16)
    a_new = product(a_two, u_mat).astype(jnp.bfloat16)
    v_mat = product(x_mat, c_one).astype(jnp.bfloat16)
    w_mat = product(a_two, v_mat).astype(jnp.bfloat16)
    c_new = (jnp.einsum("kij,klj->kil", w_mat.astype(jnp.float32), a_two.astype(jnp.float32)) + c_two.astype(jnp.float32)).astype(jnp.bfloat16)
    s_mat = product(j_two, u_mat).astype(jnp.bfloat16)
    j_new = (jnp.einsum("kji,kjl->kil", a_one.astype(jnp.float32), s_mat.astype(jnp.float32)) + j_one.astype(jnp.float32)).astype(jnp.bfloat16)
    return a_new, c_new, j_new


def doubling(element, distance):
    earlier = tuple(jnp.concatenate([jnp.zeros_like(m[:distance]), m[:-distance]], axis=0) for m in element)
    joined = combine(earlier, element)
    keep = (jnp.arange(HORIZON) >= distance)[:, None, None]
    return tuple(jnp.where(keep, new, old) for new, old in zip(joined, element))


def reference(dynamics, coupling, cost_matrix, band_offset, band_width):
    row_block = (jnp.arange(NS) // BLOCK).astype(jnp.int32)
    col_block = row_block
    lower = row_block[None, :] + band_offset[:, row_block]
    upper = lower + band_width[:, row_block]
    inside = (col_block[None, None, :] >= lower[:, :, None]) & (col_block[None, None, :] < upper[:, :, None])
    masked = jnp.where(inside, coupling, jnp.zeros_like(coupling))
    element = (dynamics, masked, cost_matrix)
    outputs = []
    for level in range(LEVELS):
        element = doubling(element, 2 ** level)
        outputs.append(jnp.stack(element, axis=1))
    return outputs[0], outputs[1]
```

```python
import jax
import jax.numpy as jnp
from jax import lax
from jax.experimental import pallas as pl
from jax.experimental.pallas import tpu as pltpu
from jax.sharding import PartitionSpec as P

BLOCK = 128
MESH = pl.DeviceIdType.MESH
F32 = jnp.float32
BF16 = jnp.bfloat16
TILE = 512

X_OWN, Y_LOW, Y_HIGH, PART_LOW, PART_HIGH, FAR_LOW, FAR_HIGH, PART_FAR, XH_LOW, XH_HIGH, XH_FAR, MATE = range(12)
J2, A1, C1, A2 = range(4)


def scan_kernel(a_in, c_in, j_in, one_out, two_out, full, c_own, j_prev, y_ref, z1, z2, g_ref, pt, sel,
                w_ref, stage, final, recv, sent, first, first_sent, out_recv, out_sent, local):
    rows, width = a_in.shape
    half = rows // 2
    tm = lax.axis_index("tm")
    panel = lax.axis_index("panel")
    z, c = tm // 2, tm % 2
    y, x = panel // 4, panel % 4
    planes = lax.axis_size("tm") // 2
    g = x // 2
    own = 1 - (g + c - 2 * g * c)

    def device(xx, yy, zz, cc):
        return (zz * 2 + cc, yy * 4 + xx)

    xo = x * own + (3 - x) * (1 - own)
    pair = 4 * g + 1 - x
    xp = pair * own + (3 - pair) * (1 - own)
    yh, yl = (y + 1) % 4, (y + 3) % 4
    yf = (y + 2) % 4
    low, high = device(x, yl, z, c), device(x, yh, z, c)
    beside = device(pair, y, z, c)
    mate = device(x, y, z, 1 - c)
    swap = device(3 - x, y, z, 1 - c)
    z_next = (z + c) % planes
    z_prev = (z + planes - (1 - g)) % planes
    following = device((3 - x) * own + x * (1 - own), y, z_next, c * own + (1 - c) * (1 - own))
    preceding = device(x * own + (3 - x) * (1 - own), y, z_prev, (1 - c) * own + c * (1 - own))
    up = device(x, y, (z + 1) % planes, c)
    down = device(x, y, (z + planes - 1) % planes, c)
    step = z * 2 + g

    def at(col, yy, part=None):
        base = (yy * 4 + col) * rows
        if part is None:
            return pl.ds(pl.multiple_of(base, 16), rows)
        return pl.ds(pl.multiple_of(base + part * half, 16), half)

    mine = at(xo, y)

    barrier = pltpu.get_barrier_semaphore()
    for other in (low, high, beside, mate, down, preceding, swap):
        pl.semaphore_signal(barrier, inc=1, device_id=other, device_id_type=MESH)
    pl.semaphore_wait(barrier, 7)

    def remote(src, dst, send_sem, recv_sem, to):
        return pltpu.make_async_remote_copy(
            src_ref=src, dst_ref=dst, send_sem=send_sem, recv_sem=recv_sem, device_id=to, device_id_type=MESH
        )

    def hand_over(src, dst, k):
        @pl.when(own == 1)
        def _():
            pltpu.make_async_copy(src, dst, first.at[k]).start()

        @pl.when(own == 0)
        def _():
            remote(src, dst, first_sent.at[k], first.at[k], swap).start()

    def hand_on(src, dst, k):
        remote(src, dst, first_sent.at[k], first.at[k], following).start()

    phys = at(x, y)
    hand_over(j_in, full.at[0, J2, phys], 0)
    hand_on(a_in, full.at[0, A1, phys], 1)
    hand_on(c_in, full.at[0, C1, phys], 2)
    hand_over(a_in, full.at[0, A2, phys], 3)
    hand_on(j_in, j_prev.at[0], 5)
    hand_over(c_in, c_own.at[0], 4)

    def got(dst, sem):
        pltpu.make_async_copy(dst, dst, sem).wait()

    def send(level, m, where, to, k):
        ref = full.at[level, m, where]
        remote(ref, ref, sent.at[level, m], recv.at[level, m, k], to).start()

    def wait(level, m, where, k):
        ref = full.at[level, m, where]
        remote(ref, ref, sent.at[level, m], recv.at[level, m, k], mate).wait_recv()

    def start_own(level, m):
        send(level, m, mine, beside, X_OWN)
        send(level, m, mine, high, Y_LOW)
        send(level, m, mine, low, Y_HIGH)
        send(level, m, mine, mate, MATE)

    def near(level, m):
        def e1():
            wait(level, m, at(xp, y), X_OWN)
            send(level, m, at(xp, y, 1), high, PART_LOW)
            send(level, m, at(xp, y, 1), low, PART_HIGH)
            send(level, m, at(xp, y), mate, MATE)

        def e2():
            wait(level, m, at(xo, yl), Y_LOW)
            send(level, m, at(xo, yl, 0), high, FAR_LOW)
            send(level, m, at(xo, yl, 0), beside, XH_LOW)
            send(level, m, at(xo, yl), mate, MATE)

        def e3():
            wait(level, m, at(xo, yh), Y_HIGH)
            send(level, m, at(xo, yh, 1), low, FAR_HIGH)
            send(level, m, at(xo, yh, 0), beside, XH_HIGH)
            send(level, m, at(xo, yh), mate, MATE)

        return [e1, e2, e3]

    def far(level, m):
        def e4():
            wait(level, m, at(xp, yl, 1), PART_LOW)
            if m % 2 == 0:
                send(level, m, at(xp, yl, 1), high, PART_FAR)
            send(level, m, at(xp, yl, 1), mate, MATE)

        def e5():
            wait(level, m, at(xp, yh, 1), PART_HIGH)
            if m % 2 == 1:
                send(level, m, at(xp, yh, 1), low, PART_FAR)
            send(level, m, at(xp, yh, 1), mate, MATE)

        def e6():
            wait(level, m, at(xo, yf, 0), FAR_LOW)
            send(level, m, at(xo, yf, 0), beside, XH_FAR)
            send(level, m, at(xo, yf, 0), mate, MATE)

        def e7():
            wait(level, m, at(xo, yf, 1), FAR_HIGH)
            send(level, m, at(xo, yf, 1), mate, MATE)

        def tail(where, k):
            def run():
                wait(level, m, where, k)
                send(level, m, where, mate, MATE)

            return run

        return [
            e4, e5, e6, e7,
            tail(at(xp, yl, 0), XH_LOW),
            tail(at(xp, yh, 0), XH_HIGH),
            tail(at(xp, yf, 1), PART_FAR),
            tail(at(xp, yf, 0), XH_FAR),
        ]

    def complete(level, m):
        wait(level, m, pl.ds(0, 8 * rows), MATE)

    def tiles(body, tile=TILE):
        def run(i, carry):
            body(pl.ds(pl.multiple_of(i * tile, tile), tile))
            return carry

        lax.fori_loop(0, width // tile, run, 0)

    def dot(left, right):
        return jnp.dot(left, right, preferred_element_type=F32)

    def dot_t(left, right):
        return lax.dot_general(left, right, (((1,), (1,)), ((), ())), preferred_element_type=F32)

    def interleave(tasks, events):
        tasks, events = list(tasks), list(events)
        total = max(len(tasks), 1)
        done = 0
        for i, task in enumerate(tasks):
            upto = (len(events) * (i + 1)) // total
            while done < upto:
                events[done]()
                done += 1
            task()
        while done < len(events):
            events[done]()
            done += 1

    def compute(level):
        a_two, j_two = full.at[level, A2], full.at[level, J2]
        a_one, c_one = full.at[level, A1], full.at[level, C1]
        keep = step >= 2**level

        def select():
            block = (yoff * 3) // 4
            block = lax.min(block, width // BLOCK - 2)
            offset = yoff * rows - block * BLOCK
            window = pl.ds(pl.multiple_of(block * BLOCK, BLOCK), 2 * BLOCK)
            r_ids = lax.broadcasted_iota(jnp.int32, (rows, 2 * BLOCK), 0)
            c_ids = lax.broadcasted_iota(jnp.int32, (rows, 2 * BLOCK), 1)
            hot = (c_ids == r_ids + offset).astype(F32).astype(BF16)

            def body(cols):
                sel[:, cols] = dot_t(hot, a_one[cols, window]).astype(BF16)

            tiles(body)

        def start_cost():
            def body(cols):
                y_ref[rows:, cols] = dot(sel[...], j_two[:, cols]).astype(BF16)

            tiles(body)

        def start_transition():
            y_ref[:rows, :] = a_two[mine, :]

        def times_c(src):
            def run():
                def body(cols):
                    g_ref[:, cols] = dot(src[...], c_one[:, cols]).astype(BF16)

                tiles(body)

            return run

        def times_j(dst):
            def run():
                def body(cols):
                    dst[:, cols] = dot(g_ref[...], j_two[:, cols]).astype(BF16)

                tiles(body)

            return run

        def last_power():
            def body(cols):
                cube = dot(g_ref[...], j_two[:, cols])
                total = y_ref[:, cols].astype(F32) - z1[:, cols].astype(F32) + z2[:, cols].astype(F32) - cube
                pt[:, cols] = total.astype(BF16)

            tiles(body)

        def new_a_j():
            def body(cols):
                both = dot(pt[...], a_one[:, cols])
                a_new = both[:rows]
                j_new = both[rows:] + j_prev[level, :, cols].astype(F32)
                stage[level, 0, :, cols] = jnp.where(keep, a_new, a_two[mine, cols].astype(F32)).astype(BF16)
                stage[level, 2, :, cols] = jnp.where(keep, j_new, j_two[mine, cols].astype(F32)).astype(BF16)

            tiles(body)

        def w_rows():
            def body(cols):
                w_ref[:, cols] = dot(pt[:rows, :], c_one[:, cols]).astype(BF16)

            tiles(body)

        def new_c():
            def body(cols):
                old = c_own[level, :, cols].astype(F32)
                c_new = dot_t(w_ref[...], a_two[cols, :]) + old
                stage[level, 1, :, cols] = jnp.where(keep, c_new, old).astype(BF16)

            tiles(body)

        powers = [start_transition, times_c(y_ref), times_j(z1), times_c(z1), times_j(z2), times_c(z2), last_power]
        return [select, start_cost], powers, new_a_j, w_rows, new_c

    yoff = y * 4 + xo

    def copied(src, dst, k):
        copy = pltpu.make_async_copy(src, dst, local.at[k])
        copy.start()
        copy.wait()

    def give_out(src, dst, level, k):
        @pl.when(own == 1)
        def _():
            pltpu.make_async_copy(src, dst, out_recv.at[level, k]).start()

        @pl.when(own == 0)
        def _():
            remote(src, dst, out_sent.at[level, k], out_recv.at[level, k], swap).start()

    def level_head(level, owns):
        owns[0]()
        start_own(level, J2)
        for event in near(level, J2):
            event()
        owns[1]()
        start_own(level, A1)
        for event in far(level, J2) + near(level, A1):
            event()

    def level_tail(level, owns):
        head, powers, new_a_j, w_rows, new_c = compute(level)
        owns[2]()
        start_own(level, C1)
        for event in far(level, A1) + near(level, C1):
            event()
        owns[3]()
        start_own(level, A2)
        complete(level, J2)
        complete(level, A1)
        interleave(head, far(level, C1) + near(level, A2))
        complete(level, C1)
        interleave(powers, far(level, A2))
        owns[4]()
        new_a_j()
        return w_rows, new_c

    owns = [
        lambda: got(full.at[0, J2, mine], first.at[0]),
        lambda: got(full.at[0, A1, mine], first.at[1]),
        lambda: got(full.at[0, C1, mine], first.at[2]),
        lambda: got(full.at[0, A2, mine], first.at[3]),
        lambda: got(j_prev.at[0], first.at[5]),
    ]
    level_head(0, owns)
    w_rows, new_c = level_tail(0, owns)
    copied(stage.at[0, 2], full.at[1, J2, mine], 0)
    copied(stage.at[0, 0], full.at[1, A2, mine], 1)

    def lift(src, dst, k):
        remote(src, dst, first_sent.at[k], first.at[k], up).start()

    lift(full.at[1, A2, mine], full.at[1, A1, mine], 6)
    lift(full.at[1, J2, mine], j_prev.at[1], 7)
    give_out(full.at[1, A2, mine], one_out.at[0], 0, 0)
    give_out(full.at[1, J2, mine], one_out.at[2], 0, 2)
    start_own(1, J2)
    w_rows()
    complete(0, A2)
    got(c_own.at[0], first.at[4])
    new_c()
    copied(stage.at[0, 1], c_own.at[1], 2)
    lift(c_own.at[1], full.at[1, C1, mine], 8)
    give_out(c_own.at[1], one_out.at[1], 0, 1)
    for event in near(1, J2):
        event()
    got(full.at[1, A1, mine], first.at[6])
    start_own(1, A1)
    for event in far(1, J2) + near(1, A1):
        event()
    w_rows, new_c = level_tail(
        1,
        [
            None,
            None,
            lambda: got(full.at[1, C1, mine], first.at[8]),
            lambda: None,
            lambda: got(j_prev.at[1], first.at[7]),
        ],
    )
    copied(stage.at[1, 0], final.at[0], 3)
    give_out(final.at[0], two_out.at[0], 1, 0)
    copied(stage.at[1, 2], final.at[2], 4)
    give_out(final.at[2], two_out.at[2], 1, 2)
    w_rows()
    complete(1, A2)
    new_c()
    copied(stage.at[1, 1], final.at[1], 5)
    give_out(final.at[1], two_out.at[1], 1, 1)

    for level, out in ((0, one_out), (1, two_out)):
        for k in range(3):
            got(out.at[k], out_recv.at[level, k])

            @pl.when(own == 0)
            def _():
                remote(final.at[k], out.at[k], out_sent.at[level, k], out_recv.at[level, k], swap).wait_send()

    for k in (0, 3, 4):

        @pl.when(own == 0)
        def _():
            remote(a_in, c_own.at[0], first_sent.at[k], first.at[k], swap).wait_send()

    for k in (1, 2, 5, 6, 7, 8):
        remote(a_in, c_own.at[0], first_sent.at[k], first.at[k], up).wait_send()
    for level in range(2):
        for m in range(4):
            ref = full.at[level, m, pl.ds(0, 15 * rows)]
            remote(ref, ref, sent.at[level, m], recv.at[level, m, 0], mate).wait_send()


def scan_levels(a, c, j):
    rows, width = a.shape
    vmem = lambda *shape: pltpu.VMEM(shape, BF16)
    dma = lambda *shape: pltpu.SemaphoreType.DMA(shape)
    wide = (2 * rows, width)
    out = jax.ShapeDtypeStruct((3, rows, width), BF16)
    return pl.pallas_call(
        scan_kernel,
        out_shape=(out, out),
        in_specs=[pl.BlockSpec(memory_space=pl.ANY)] * 3,
        out_specs=[pl.BlockSpec(memory_space=pl.ANY)] * 2,
        scratch_shapes=[
            vmem(2, 4, width, width),
            vmem(2, rows, width),
            vmem(2, rows, width),
            vmem(*wide), vmem(*wide), vmem(*wide), vmem(*wide), vmem(*wide),
            vmem(rows, width),
            vmem(rows, width),
            vmem(2, 3, rows, width),
            vmem(3, rows, width),
            dma(2, 4, 12),
            dma(2, 4),
            dma(9),
            dma(9),
            dma(2, 3),
            dma(2, 3),
            dma(6),
        ],
        compiler_params=pltpu.CompilerParams(
            collective_id=0, has_side_effects=True, vmem_limit_bytes=60 * 2**20
        ),
        name="scan_levels",
    )(a, c, j)


def shards(dynamics, coupling, cost_matrix, band_offset, band_width):
    rows = dynamics.shape[1]
    width = dynamics.shape[2]
    first = lax.axis_index("panel") * rows
    row_block = (first + jnp.arange(rows, dtype=jnp.int32)) // BLOCK
    block_ids = jnp.arange(width // BLOCK, dtype=jnp.int32)
    picked = row_block[:, None] == block_ids[None, :]
    offsets = jnp.sum(jnp.where(picked, band_offset[0][None, :], 0), axis=1)
    widths = jnp.sum(jnp.where(picked, band_width[0][None, :], 0), axis=1)
    col_block = jnp.arange(width, dtype=jnp.int32) // BLOCK
    lower = row_block + offsets
    inside = (col_block[None, :] >= lower[:, None]) & (
        col_block[None, :] < (lower + widths)[:, None]
    )
    c_start = jnp.where(inside, coupling[0], jnp.zeros_like(coupling[0]))
    one, two = scan_levels(dynamics[0], c_start, cost_matrix[0])
    return one[None], two[None]


def solution(mesh):
    in_specs = (
        P("tm", "panel", None),
        P("tm", "panel", None),
        P("tm", "panel", None),
        P("tm", None),
        P("tm", None),
    )
    out_specs = (P("tm", None, "panel", None), P("tm", None, "panel", None))
    return jax.shard_map(shards, mesh=mesh, in_specs=in_specs, out_specs=out_specs, check_vma=False)
```

```python
import jax
import jax.numpy as jnp
from jax import lax
from jax.experimental import pallas as pl
from jax.experimental.pallas import tpu as pltpu
from jax.sharding import PartitionSpec as P

BLOCK = 128
MESH = pl.DeviceIdType.MESH
F32 = jnp.float32
BF16 = jnp.bfloat16
SPAN = 5
TILE = 4 * BLOCK

X_OWN, Y_LOW, Y_HIGH, PART_LOW, PART_HIGH, FAR_LOW, FAR_HIGH, PART_FAR, XH_LOW, XH_HIGH, XH_FAR, MATE = range(12)
J2, A1, C1, A2 = range(4)
FROM_LOW = (True, False, False, True)


def scan_kernel(offset_in, width_in, a_in, c_in, j_in, one_out, two_out, full, c_own, j_prev, y_ref, z1, z2, g_ref,
                pt, sel, w_ref, stage, final, banded, recv, sent, first, first_sent, out_recv, out_sent, local):
    rows, width = a_in.shape
    half = rows // 2
    tm = lax.axis_index("tm")
    panel = lax.axis_index("panel")
    z, c = tm // 2, tm % 2
    y, x = panel // 4, panel % 4
    planes = lax.axis_size("tm") // 2
    g = x // 2
    own = 1 - (g + c - 2 * g * c)

    def device(xx, yy, zz, cc):
        return (zz * 2 + cc, yy * 4 + xx)

    xo = x * own + (3 - x) * (1 - own)
    pair = 4 * g + 1 - x
    xp = pair * own + (3 - pair) * (1 - own)
    yh, yl = (y + 1) % 4, (y + 3) % 4
    yf = (y + 2) % 4
    low, high = device(x, yl, z, c), device(x, yh, z, c)
    beside = device(pair, y, z, c)
    mate = device(x, y, z, 1 - c)
    swap = device(3 - x, y, z, 1 - c)
    z_next = (z + c) % planes
    z_prev = (z + planes - (1 - g)) % planes
    following = device((3 - x) * own + x * (1 - own), y, z_next, c * own + (1 - c) * (1 - own))
    preceding = device(x * own + (3 - x) * (1 - own), y, z_prev, (1 - c) * own + c * (1 - own))
    up = device(x, y, (z + 1) % planes, c)
    down = device(x, y, (z + planes - 1) % planes, c)
    step = z * 2 + g

    def at(col, yy, part=None):
        q = yy * 4 + col
        if part is None:
            return q, pl.ds(pl.multiple_of(q * rows, 16), rows)
        return q, pl.ds(pl.multiple_of(q * rows + part * half, 16), half)

    def span(q):
        block = lax.max(lax.min((q * 3) // 4 - 1, width // BLOCK - SPAN), 0)
        return pl.ds(pl.multiple_of(block * BLOCK, BLOCK), SPAN * BLOCK)

    def panel_ref(level, m, where):
        q, some = where
        if (level, m) == (0, C1):
            return full.at[0, C1, some, span(q)]
        return full.at[level, m, some]

    mine = at(xo, y)[1]
    raw = pltpu.make_async_copy(c_in, banded.at[0], local.at[5])
    raw.start()

    barrier = pltpu.get_barrier_semaphore()
    for other in (low, high, beside, mate, down, preceding, swap):
        pl.semaphore_signal(barrier, inc=1, device_id=other, device_id_type=MESH)
    pl.semaphore_wait(barrier, 7)

    def remote(src, dst, send_sem, recv_sem, to):
        return pltpu.make_async_remote_copy(
            src_ref=src, dst_ref=dst, send_sem=send_sem, recv_sem=recv_sem, device_id=to, device_id_type=MESH
        )

    yoff = y * 4 + xo

    def copied(src, dst, k):
        copy = pltpu.make_async_copy(src, dst, local.at[k])
        copy.start()
        copy.wait()

    def hand_over(src, dst, k):
        @pl.when(own == 1)
        def _():
            pltpu.make_async_copy(src, dst, first.at[k]).start()

        @pl.when(own == 0)
        def _():
            remote(src, dst, first_sent.at[k], first.at[k], swap).start()

    def hand_on(src, dst, k):
        remote(src, dst, first_sent.at[k], first.at[k], following).start()

    phys = at(x, y)[1]
    hand_over(j_in, full.at[0, J2, phys], 0)
    hand_on(a_in, full.at[0, A1, phys], 1)

    def hand_coupling():
        block = (panel * 3) // 4
        after = lax.min(block + 1, width // BLOCK - 1)
        r_ids = lax.broadcasted_iota(jnp.int32, (rows, width), 0) + panel * rows
        c_ids = lax.broadcasted_iota(jnp.int32, (rows, width), 1)
        later = r_ids >= (block + 1) * BLOCK
        low_0 = (block + offset_in[0, block]) * BLOCK
        low_1 = (block + 1 + offset_in[0, after]) * BLOCK
        start = jnp.where(later, low_1, low_0)
        stop = jnp.where(later, low_1 + width_in[0, after] * BLOCK, low_0 + width_in[0, block] * BLOCK)
        raw.wait()
        values = banded[0].astype(F32)
        stage[0, 1] = jnp.where((c_ids >= start) & (c_ids < stop), values, 0.0).astype(BF16)
        copied(stage.at[0, 1], banded.at[1], 4)
        hand_on(banded.at[1, :, span(panel)], full.at[0, C1, phys, span(panel)], 2)
        hand_over(a_in, full.at[0, A2, phys], 3)
        hand_on(j_in, j_prev.at[0], 5)
        hand_over(banded.at[1], c_own.at[0], 4)

    def clear_outside():
        for q in range(width // rows):
            left = max(min((q * 3) // 4 - 1, width // BLOCK - SPAN), 0) * BLOCK
            right = left + SPAN * BLOCK
            if left:
                full[0, C1, q * rows : (q + 1) * rows, :left] = jnp.zeros((rows, left), BF16)
            if right < width:
                full[0, C1, q * rows : (q + 1) * rows, right:] = jnp.zeros((rows, width - right), BF16)

    def got(dst, sem):
        pltpu.make_async_copy(dst, dst, sem).wait()

    def send(level, m, where, to, k):
        ref = panel_ref(level, m, where)
        remote(ref, ref, sent.at[level, m], recv.at[level, m, k], to).start()

    def wait(level, m, where, k):
        ref = panel_ref(level, m, where)
        remote(ref, ref, sent.at[level, m], recv.at[level, m, k], mate).wait_recv()

    def start_own(level, m):
        here = at(xo, y)
        send(level, m, here, beside, X_OWN)
        send(level, m, here, high, Y_LOW)
        send(level, m, here, low, Y_HIGH)
        send(level, m, here, mate, MATE)

    def near(level, m):
        def e1():
            wait(level, m, at(xp, y), X_OWN)
            send(level, m, at(xp, y, 1), high, PART_LOW)
            send(level, m, at(xp, y, 1), low, PART_HIGH)
            send(level, m, at(xp, y), mate, MATE)

        def e2():
            wait(level, m, at(xo, yl), Y_LOW)
            send(level, m, at(xo, yl, 0), high, FAR_LOW)
            send(level, m, at(xo, yl, 0), beside, XH_LOW)
            send(level, m, at(xo, yl), mate, MATE)

        def e3():
            wait(level, m, at(xo, yh), Y_HIGH)
            send(level, m, at(xo, yh, 1), low, FAR_HIGH)
            send(level, m, at(xo, yh, 0), beside, XH_HIGH)
            send(level, m, at(xo, yh), mate, MATE)

        return [e1, e2, e3]

    def far(level, m):
        def e4():
            wait(level, m, at(xp, yl, 1), PART_LOW)
            if FROM_LOW[m]:
                send(level, m, at(xp, yl, 1), high, PART_FAR)

        def e5():
            wait(level, m, at(xp, yh, 1), PART_HIGH)
            if not FROM_LOW[m]:
                send(level, m, at(xp, yh, 1), low, PART_FAR)

        def e6():
            wait(level, m, at(xo, yf, 0), FAR_LOW)
            send(level, m, at(xo, yf, 0), beside, XH_FAR)

        def e7():
            wait(level, m, at(xo, yf, 1), FAR_HIGH)
            send(level, m, at(xo, yf), mate, MATE)

        return [e4, e5, e6, e7]

    def crossed(level, m):
        def e8():
            wait(level, m, at(xp, yl, 0), XH_LOW)
            send(level, m, at(xp, yl), mate, MATE)

        def e9():
            wait(level, m, at(xp, yh, 0), XH_HIGH)
            send(level, m, at(xp, yh), mate, MATE)

        def e10():
            wait(level, m, at(xp, yf, 1), PART_FAR)
            wait(level, m, at(xp, yf, 0), XH_FAR)
            send(level, m, at(xp, yf), mate, MATE)

        return [e8, e9, e10]

    def complete(level, m):
        wait(level, m, (0, pl.ds(0, 8 * rows)), MATE)

    def tiles(body):
        body(pl.ds(0, width))

    def dot(left, right):
        return jnp.dot(left, right, preferred_element_type=F32)

    def dot_t(left, right):
        return lax.dot_general(left, right, (((1,), (1,)), ((), ())), preferred_element_type=F32)

    def interleave(tasks, events):
        tasks, events = list(tasks), list(events)
        total = max(len(tasks), 1)
        done = 0
        for i, task in enumerate(tasks):
            upto = (len(events) * (i + 1)) // total
            while done < upto:
                events[done]()
                done += 1
            task()
        while done < len(events):
            events[done]()
            done += 1

    def compute(level):
        a_two, j_two = full.at[level, A2], full.at[level, J2]
        a_one, c_one = full.at[level, A1], full.at[level, C1]
        keep = step >= 2**level

        def select():
            block = (yoff * 3) // 4
            block = lax.min(block, width // BLOCK - 2)
            offset = yoff * rows - block * BLOCK
            window = pl.ds(pl.multiple_of(block * BLOCK, BLOCK), 2 * BLOCK)
            r_ids = lax.broadcasted_iota(jnp.int32, (rows, 2 * BLOCK), 0)
            c_ids = lax.broadcasted_iota(jnp.int32, (rows, 2 * BLOCK), 1)
            hot = (c_ids == r_ids + offset).astype(F32).astype(BF16)

            def body(cols):
                sel[:, cols] = dot_t(hot, a_one[cols, window]).astype(BF16)

            tiles(body)

        def start_cost():
            def body(cols):
                y_ref[rows:, cols] = dot(sel[...], j_two[:, cols]).astype(BF16)

            tiles(body)

        def start_transition():
            y_ref[:rows, :] = a_two[mine, :]

        def into_c(src, dst):
            if level:
                dst[...] = dot(src[...], c_one[...]).astype(BF16)
                return
            deep = TILE + 3 * BLOCK
            for left in range(0, width, TILE):
                top = min(max(left - 2 * BLOCK, 0), width - deep)
                rows_in, cols = slice(top, top + deep), slice(left, left + TILE)
                dst[:, cols] = dot(src[:, rows_in], c_one[rows_in, cols]).astype(BF16)

        def times_c(src):
            return lambda: into_c(src, g_ref)

        def times_j(dst):
            def run():
                def body(cols):
                    dst[:, cols] = dot(g_ref[...], j_two[:, cols]).astype(BF16)

                tiles(body)

            return run

        def last_power():
            def body(cols):
                cube = dot(g_ref[...], j_two[:, cols])
                total = y_ref[:, cols].astype(F32) - z1[:, cols].astype(F32) + z2[:, cols].astype(F32) - cube
                pt[:, cols] = total.astype(BF16)

            tiles(body)

        def new_a_j():
            def body(cols):
                both = dot(pt[...], a_one[:, cols])
                a_new = both[:rows]
                j_new = both[rows:] + j_prev[level, :, cols].astype(F32)
                stage[level, 0, :, cols] = jnp.where(keep, a_new, a_two[mine, cols].astype(F32)).astype(BF16)
                stage[level, 2, :, cols] = jnp.where(keep, j_new, j_two[mine, cols].astype(F32)).astype(BF16)

            tiles(body)

        def w_rows():
            into_c(pt.at[:rows], w_ref)

        def new_c():
            def body(cols):
                old = c_own[level, :, cols].astype(F32)
                c_new = dot_t(w_ref[...], a_two[cols, :]) + old
                stage[level, 1, :, cols] = jnp.where(keep, c_new, old).astype(BF16)

            tiles(body)

        powers = [start_transition, times_c(y_ref), times_j(z1), times_c(z1), times_j(z2), times_c(z2), last_power]
        return [select, start_cost], powers, new_a_j, w_rows, new_c

    def give_out(src, dst, level, k):
        @pl.when(own == 1)
        def _():
            pltpu.make_async_copy(src, dst, out_recv.at[level, k]).start()

        @pl.when(own == 0)
        def _():
            remote(src, dst, out_sent.at[level, k], out_recv.at[level, k], swap).start()

    def run_all(events):
        for event in events:
            event()

    def level_head(level, owns):
        owns[1]()
        start_own(level, A1)
        run_all(near(level, J2))

    def level_tail(level, owns):
        head, powers, new_a_j, w_rows, new_c = compute(level)
        owns[2]()
        start_own(level, C1)
        run_all(far(level, J2) + near(level, A1) + crossed(level, J2))
        owns[3]()
        start_own(level, A2)
        run_all(far(level, A1) + near(level, C1) + crossed(level, A1))
        complete(level, J2)
        complete(level, A1)
        interleave(head, far(level, C1) + near(level, A2) + crossed(level, C1))
        complete(level, C1)
        interleave(powers, far(level, A2) + crossed(level, A2))
        owns[4]()
        new_a_j()
        return w_rows, new_c

    owns = [
        lambda: got(full.at[0, J2, mine], first.at[0]),
        lambda: got(full.at[0, A1, mine], first.at[1]),
        lambda: got(full.at[0, C1, mine, span(yoff)], first.at[2]),
        lambda: got(full.at[0, A2, mine], first.at[3]),
        lambda: got(j_prev.at[0], first.at[5]),
    ]
    owns[0]()
    start_own(0, J2)
    hand_coupling()
    clear_outside()
    level_head(0, owns)
    w_rows, new_c = level_tail(0, owns)
    copied(stage.at[0, 2], full.at[1, J2, mine], 0)
    copied(stage.at[0, 0], full.at[1, A2, mine], 1)

    def lift(src, dst, k):
        remote(src, dst, first_sent.at[k], first.at[k], up).start()

    lift(full.at[1, A2, mine], full.at[1, A1, mine], 6)
    give_out(full.at[1, A2, mine], one_out.at[0], 0, 0)
    give_out(full.at[1, J2, mine], one_out.at[2], 0, 2)
    start_own(1, J2)
    w_rows()
    complete(0, A2)
    got(c_own.at[0], first.at[4])
    new_c()
    copied(stage.at[0, 1], c_own.at[1], 2)
    lift(c_own.at[1], full.at[1, C1, mine], 8)
    lift(full.at[1, J2, mine], j_prev.at[1], 7)
    give_out(c_own.at[1], one_out.at[1], 0, 1)
    level_head(1, [None, lambda: got(full.at[1, A1, mine], first.at[6])])
    w_rows, new_c = level_tail(
        1,
        [
            None,
            None,
            lambda: got(full.at[1, C1, mine], first.at[8]),
            lambda: None,
            lambda: got(j_prev.at[1], first.at[7]),
        ],
    )
    copied(stage.at[1, 0], final.at[0], 3)
    give_out(final.at[0], two_out.at[0], 1, 0)
    copied(stage.at[1, 2], final.at[2], 4)
    give_out(final.at[2], two_out.at[2], 1, 2)
    w_rows()
    complete(1, A2)
    new_c()
    copied(stage.at[1, 1], final.at[1], 5)
    give_out(final.at[1], two_out.at[1], 1, 1)

    for level, out in ((0, one_out), (1, two_out)):
        for k in range(3):
            got(out.at[k], out_recv.at[level, k])

            @pl.when(own == 0)
            def _():
                remote(final.at[k], out.at[k], out_sent.at[level, k], out_recv.at[level, k], swap).wait_send()

    for k in (0, 3, 4):

        @pl.when(own == 0)
        def _():
            remote(a_in, c_own.at[0], first_sent.at[k], first.at[k], swap).wait_send()

    for k in (1, 5, 6, 7, 8):
        remote(a_in, c_own.at[0], first_sent.at[k], first.at[k], up).wait_send()
    thin = full.at[0, C1, phys, span(panel)]
    remote(thin, thin, first_sent.at[2], first.at[2], up).wait_send()
    for level in range(2):
        for m in range(4):
            ref = panel_ref(level, m, (0, pl.ds(0, 15 * rows)))
            remote(ref, ref, sent.at[level, m], recv.at[level, m, 0], mate).wait_send()


def scan_levels(offset, reach, a, c, j):
    rows, width = a.shape
    vmem = lambda *shape: pltpu.VMEM(shape, BF16)
    dma = lambda *shape: pltpu.SemaphoreType.DMA(shape)
    wide = (2 * rows, width)
    out = jax.ShapeDtypeStruct((3, rows, width), BF16)
    return pl.pallas_call(
        scan_kernel,
        out_shape=(out, out),
        in_specs=[pl.BlockSpec(memory_space=pltpu.SMEM)] * 2 + [pl.BlockSpec(memory_space=pl.ANY)] * 3,
        out_specs=[pl.BlockSpec(memory_space=pl.ANY)] * 2,
        scratch_shapes=[
            vmem(2, 4, width, width),
            vmem(2, rows, width),
            vmem(2, rows, width),
            vmem(*wide), vmem(*wide), vmem(*wide), vmem(*wide), vmem(*wide),
            vmem(rows, width),
            vmem(rows, width),
            vmem(2, 3, rows, width),
            vmem(3, rows, width),
            vmem(2, rows, width),
            dma(2, 4, 12),
            dma(2, 4),
            dma(9),
            dma(9),
            dma(2, 3),
            dma(2, 3),
            dma(6),
        ],
        compiler_params=pltpu.CompilerParams(
            collective_id=0, has_side_effects=True, vmem_limit_bytes=60 * 2**20
        ),
        name="scan_levels",
    )(offset, reach, a, c, j)


def shards(dynamics, coupling, cost_matrix, band_offset, band_width):
    one, two = scan_levels(band_offset, band_width, dynamics[0], coupling[0], cost_matrix[0])
    return one[None], two[None]


def solution(mesh):
    in_specs = (
        P("tm", "panel", None),
        P("tm", "panel", None),
        P("tm", "panel", None),
        P("tm", None),
        P("tm", None),
    )
    out_specs = (P("tm", None, "panel", None), P("tm", None, "panel", None))
    return jax.shard_map(shards, mesh=mesh, in_specs=in_specs, out_specs=out_specs, check_vma=False)
```
